512 devices in a mesh: freq: 8 (over x, core), space: 64 (over z, y).
Axes of the slice: x: 4, y: 8, z: 8, core: 2. Of those that a mesh axis runs over, the one named last changes fastest.
Arguments:
- rhs: float32 [2, 5, 4096, 1024], P(None, None, ('freq', 'space')), parts along dimension 2, may hold values from -12 to 12
- inv_diag: float32 [2, 5, 5, 4096, 1024], P(None, None, None, ('freq', 'space')), parts along dimension 3
- face_coef: float32 [4, 4096, 1024], P(None, ('freq', 'space')), parts along dimension 1, may hold values from 0.6 to 1.8
- flux_jac: float32 [2, 5, 5], replicated, may hold values from -1.8 to 1.8
- press_weights: float32 [5], replicated, may hold values from -4 to 4
- surface_cells: int32 [32768], P('space'), may hold values from 0 to 8191, as said below
- interface_slot: int32 [32768], P('space'), may hold values from 0 to 32767, as said below
- mode_shapes: float32 [32768, 192], P('space'), may hold values from -0.09375 to 0.09375
Outputs:
- state: float32 [2, 5, 4096, 1024], P(None, None, ('freq', 'space')), parts along dimension 2
- forces: float32 [2, 1536], P(None, ('freq', 'space')), parts along dimension 1
The draws below stay inside these ranges and needn't reach their ends.
There are 8 independent parts, one for each index of `freq`. The reference program is written for one: setup_inputs(seed, part) draws one part's arguments, and reference() takes and returns one part's arrays. A program takes and returns all parts, laid end to end along the dimension named above; an argument that names none is the same for every part. Nothing has to cross between parts.
Inputs may be any that keep to these rules, and one draw needn't show every extreme that they name: `surface_cells`: the 512 entries held by one device are distinct cell indices of that device; on some device they include both its first and its last cell. `interface_slot`: A permutation of all 32768 interface indices; the owner of index i is device i // 512 of space, and each device holds exactly the same number of rows of every owner.
All inputs are finite; a program needn't handle non-finite values.
Results may differ from the reference program's by a relative error of at most 0.0003.
Values sent between devices are 32-bit elements; how exact they have to be, the bound alone decides.
No kernel may reach another device: no remote copies, remote signals or barrier semaphores. Data moves between devices by JAX's collectives and lax.ppermute only.
A program may use at most 64 MiB of HBM per device.

```python
import jax
import jax.numpy as jnp
from jax import lax

COMP = 5
NP = 8
NQ = 1024
SD = 512
MODES = 192
ITERS = 8
NPT = 512
SURF = 32768
N_SPACE = 64


def draw_inv_diag(key, part):
    key_scale = jax.random.fold_in(key, 11)
    key_noise = jax.random.fold_in(key, 12)
    key_phase = jax.random.fold_in(key, 13)
    scales = jnp.exp(jax.random.uniform(key_scale, (NPT, NQ), jnp.float32, jnp.log(0.25), jnp.log(0.5)))
    noise = 0.25 * jax.random.normal(key_noise, (2, 5, 5, NPT, NQ), jnp.float32)
    identity = jnp.eye(5, dtype=jnp.float32)[:, :, None, None]
    phases = jax.random.uniform(key_phase, (NPT, NQ), jnp.float32, -0.6, 0.6)
    diagonal = jnp.stack([identity * jnp.ones((NPT, NQ), jnp.float32), identity * phases])
    return (scales * (diagonal + noise)).astype(jnp.float32)


def draw_surface_cells(key, part):
    total = NP * NQ
    device_keys = jax.random.split(jax.random.fold_in(key, 21), N_SPACE)
    drawn = jax.vmap(lambda single: jax.random.permutation(single, total)[:SD])(device_keys)
    chosen = jax.random.randint(jax.random.fold_in(key, 22), (), 0, N_SPACE)
    inner = jax.random.permutation(jax.random.fold_in(key, 23), total - 2)[:SD - 2].astype(jnp.int32) + 1
    ends = jnp.array([0, total - 1], dtype=jnp.int32)
    special = jax.random.permutation(jax.random.fold_in(key, 24), jnp.concatenate([ends, inner]))
    rows = jnp.arange(N_SPACE, dtype=jnp.int32)[:, None]
    picks = jnp.where(rows == chosen, special[None].astype(jnp.int32), drawn.astype(jnp.int32))
    return picks.reshape(-1).astype(jnp.int32)


def draw_interface_slot(key, part):
    share = SD // N_SPACE
    owner_keys = jax.random.split(jax.random.fold_in(key, 31), N_SPACE)
    owned = jax.vmap(lambda single: jax.random.permutation(single, SD))(owner_keys)
    owned = owned.astype(jnp.int32) + (jnp.arange(N_SPACE, dtype=jnp.int32) * SD)[:, None]
    blocks = owned.reshape(N_SPACE, N_SPACE, share).transpose(1, 0, 2).reshape(N_SPACE, SD)
    source_keys = jax.random.split(jax.random.fold_in(key, 32), N_SPACE)
    shuffled = jax.vmap(lambda single, values: jax.random.permutation(single, values))(source_keys, blocks)
    return shuffled.reshape(-1).astype(jnp.int32)


def raised(result, key, source, target, parts, factor):
    owner, partner = [(jnp.arange(result.shape[dim]) // (result.shape[dim] // parts)).reshape([-1 if axis == dim else 1 for axis in range(result.ndim)]) for dim in (source, target)]
    chosen = jax.random.permutation(key, parts)[partner]
    strong = (owner == chosen) | (owner == (partner + parts // 2) % parts)
    return jnp.where(strong, factor * result, result)


def level_of(stream_key, shape, cuts, least, high):
    def one(position, blocks):
        heights = jax.random.uniform(jax.random.fold_in(jax.random.fold_in(stream_key, 6), position), (blocks,), jnp.float32, least / len(cuts), high / len(cuts))
        return jnp.repeat(jnp.exp(heights), shape[position] // blocks).reshape((-1,) + (1,) * (len(shape) - position - 1))

    level = one(*cuts[0])
    for cut in cuts[1:]:
        level = level * one(*cut)
    return level


def gaussian(key, extent, spread, limit, pieces=(), kind=jnp.bfloat16):
    level = level_of(key, extent, pieces, -0.22, 0.18) if pieces else 1.0
    drawn = jax.random.normal(key, extent, jnp.float32) * spread * level
    return jnp.minimum(jnp.maximum(drawn, -limit), limit).astype(kind)


def bell_draw_with(key, shape, width, limit, cuts, heavy, held_as=jnp.bfloat16):
    result = width * jax.random.normal(key, shape, jnp.float32)
    if cuts:
        result = result * level_of(key, shape, cuts, -0.22, 0.18)
    return jnp.clip(raised(result, jax.random.fold_in(key, 3), *heavy), -limit, limit).astype(held_as)


def setup_inputs(seed: int = 0, part: int = 0) -> dict:
    key_list = jax.random.split(jax.random.key(seed), 9)
    part_keys = jax.random.split(jax.random.fold_in(key_list[8], part), 9)
    rhs = gaussian(part_keys[0], (2, COMP, NPT, NQ), 2.0, 12.0, ((2, 64),), jnp.float32)
    inv_diag = draw_inv_diag(jax.random.fold_in(jax.random.fold_in(key_list[8], part), 71), part)
    face_coef = jnp.clip(0.6 + 1.1999999 * jax.random.uniform(part_keys[2], (4, NPT, NQ), jnp.float32) ** level_of(part_keys[2], (4, NPT, NQ), ((1, 64),), -0.2, 0.2), 0.6, 1.8)
    flux_jac = gaussian(key_list[3], (2, COMP, COMP), 0.3, 1.8, (), jnp.float32)
    press_weights = gaussian(key_list[4], (COMP,), 1.0, 4.0, (), jnp.float32)
    surface_cells = draw_surface_cells(jax.random.fold_in(key_list[8], 71), part)
    interface_slot = draw_interface_slot(jax.random.fold_in(key_list[8], 71), part)
    mode_shapes = bell_draw_with(key_list[7], (SURF, MODES), SURF ** -0.5, 0.09375, ((0, 64),), (0, 1, 64, 4.0), jnp.float32)
    return dict(rhs=rhs, inv_diag=inv_diag, face_coef=face_coef, flux_jac=flux_jac, press_weights=press_weights, surface_cells=surface_cells, interface_slot=interface_slot, mode_shapes=mode_shapes)


def block_apply(inv_diag, vector):
    real_part = jnp.sum(inv_diag[0] * vector[0][None], axis=1) - jnp.sum(inv_diag[1] * vector[1][None], axis=1)
    imag_part = jnp.sum(inv_diag[0] * vector[1][None], axis=1) + jnp.sum(inv_diag[1] * vector[0][None], axis=1)
    return jnp.stack([real_part, imag_part])


def couple(extended, face_coef, flux_jac):
    middle = extended[:, :, 1:-1, :]
    along_planes = face_coef[0] * extended[:, :, 2:, :] + face_coef[1] * extended[:, :, :-2, :]
    padded = jnp.pad(middle, ((0, 0), (0, 0), (0, 0), (1, 1)))
    along_cells = face_coef[2] * padded[..., 2:] + face_coef[3] * padded[..., :-2]
    mixed = jnp.einsum('kj,rjpq->rkpq', flux_jac[0], along_planes, precision=lax.Precision.HIGHEST)
    return mixed + jnp.einsum('kj,rjpq->rkpq', flux_jac[1], along_cells, precision=lax.Precision.HIGHEST)


def sweep(extended, inv_diag, rhs, face_coef, flux_jac):
    return block_apply(inv_diag, rhs + couple(extended, face_coef, flux_jac))


def reference(rhs, inv_diag, face_coef, flux_jac, press_weights, surface_cells, interface_slot, mode_shapes):
    state = block_apply(inv_diag, rhs)
    for sweep_index in range(ITERS):
        padded = jnp.pad(state, ((0, 0), (0, 0), (1, 1), (0, 0)))
        state = sweep(padded, inv_diag, rhs, face_coef, flux_jac)
    cells = state.reshape(2, COMP, N_SPACE, NP * NQ)
    pressure = jnp.sum(press_weights[None, :, None, None] * cells, axis=1)
    picks = surface_cells.reshape(N_SPACE, SD)
    surface = jnp.take_along_axis(pressure, picks[None], axis=2)
    placed = jnp.zeros((2, SURF), jnp.float32).at[:, interface_slot].set(surface.reshape(2, SURF))
    forces = jnp.dot(placed, mode_shapes, precision=lax.Precision.HIGHEST, preferred_element_type=jnp.float32)
    return state, forces
```

```python
import jax
import jax.numpy as jnp
from jax import lax
from jax.experimental import pallas as pl
from jax.experimental.pallas import tpu as pltpu
from jax.sharding import PartitionSpec as P

INTERPRET = False
HI = lax.Precision.HIGHEST
F32 = jnp.float32
BLK = 50
RHS = 50
FAC = 60
NF = 64
LANES = 128
MIB = 1 << 20


def tile_iota(dim):
    return lax.broadcasted_iota(jnp.int32, (8, LANES), dim)


def matvec(blk, vec):
    out = []
    for r in range(2):
        for k in range(5):
            acc = None
            for j in range(5):
                br, bi = blk(k * 5 + j), blk(25 + k * 5 + j)
                if r == 0:
                    term = br * vec[j] - bi * vec[5 + j]
                else:
                    term = br * vec[5 + j] + bi * vec[j]
                acc = term if acc is None else acc + term
            out.append(acc)
    return out


def next_cell(x):
    rolled = pltpu.roll(x, LANES - 1, 1)
    return jnp.where(tile_iota(1) == LANES - 1, pltpu.roll(rolled, 7, 0), rolled)


def prev_cell(x):
    rolled = pltpu.roll(x, 1, 1)
    return jnp.where(tile_iota(1) == 0, pltpu.roll(rolled, 1, 0), rolled)


def start_state(cx, st, plane):
    c, e = plane + 2, plane + 3
    new = matvec(lambda f: cx[f, c], [cx[RHS + f, c] for f in range(10)])
    for f in range(10):
        st[f, e] = new[f]


def advance(cx, st, flux, level, plane, out=None):
    c, e = plane + 2, plane + 3
    base = (level - 1) * 10
    f0, f1, f2, f3 = [cx[FAC + n, c] for n in range(4)]
    last = (tile_iota(0) == 7) & (tile_iota(1) == LANES - 1)
    first = (tile_iota(0) == 0) & (tile_iota(1) == 0)
    f2 = jnp.where(last, 0.0, f2)
    f3 = jnp.where(first, 0.0, f3)
    vec = []
    for r in range(2):
        across, along = [], []
        for j in range(5):
            n = base + r * 5 + j
            here = st[n, e]
            across.append(f0 * st[n, e + 1] + f1 * st[n, e - 1])
            along.append(f2 * next_cell(here) + f3 * prev_cell(here))
        for k in range(5):
            acc = cx[RHS + r * 5 + k, c]
            for j in range(5):
                acc = acc + flux[0, k, j] * across[j]
            for j in range(5):
                acc = acc + flux[1, k, j] * along[j]
            vec.append(acc)
    new = matvec(lambda f: cx[f, c], vec)
    for f in range(10):
        if out is None:
            st[level * 10 + f, e] = new[f]
        else:
            out[f, plane] = new[f]


def run(planes, body):
    for low, high in planes:
        if low == high:
            body(low)
        else:

            @pl.loop(low, high + 1)
            def _(plane):
                body(plane)


def plane_copies(source, target, sems, first, count, offset, at):
    copies = []
    for j in range(8):
        copies.append(
            pltpu.make_async_copy(
                source.at[:, first : first + count, j * LANES : (j + 1) * LANES],
                target.at[offset : offset + source.shape[0], at : at + count, j, :],
                sems,
            )
        )
    return copies


def pack_kernel(rhs, inv, face, low, high, edge, sems):
    copies = []
    for side, (target, first, inner) in enumerate(((low, 0, 2), (high, 6, 5))):
        copies += plane_copies(inv, target, sems.at[side], first, 2, 0, 0)
        copies += plane_copies(rhs, target, sems.at[side], first, 2, RHS, 0)
        copies += plane_copies(face, target, sems.at[side], first, 2, FAC, 0)
        copies += plane_copies(inv, edge, sems.at[side], inner, 1, 0, side)
        copies += plane_copies(rhs, edge, sems.at[side], inner, 1, RHS, side)
    for copy in copies:
        copy.start()
    for copy in copies:
        copy.wait()
    for side, target in enumerate((low, high)):
        new = matvec(lambda f: edge[f, side], [edge[RHS + f, side] for f in range(10)])
        for f in range(10):
            target[NF + f // 2, f % 2] = new[f]


def inner_kernel(flux, rhs, inv, face, cx, st, sems):
    copies = (
        plane_copies(inv, cx, sems.at[0], 0, 8, 0, 2)
        + plane_copies(rhs, cx, sems.at[0], 0, 8, RHS, 2)
        + plane_copies(face, cx, sems.at[0], 0, 8, FAC, 2)
    )
    for copy in copies:
        copy.start()
    for copy in copies:
        copy.wait()
    run([(0, 7)], lambda p: start_state(cx, st, p))
    for level in (1, 2, 3):
        run([(level, 7 - level)], lambda p: advance(cx, st, flux, level, p))


def middle_kernel(flux, got_low, got_high, cx_in, st_in, cx, st, low, high):
    del cx_in, st_in
    @pl.loop(0, NF)
    def _(f):
        for p in range(2):
            cx[f, p] = got_low[f, p]
            cx[f, 10 + p] = got_high[f, p]

    for f in range(10):
        st[f, 0] = got_low[NF + f // 2, f % 2]
        st[f, 13] = got_high[NF + f // 2, f % 2]
    run([(-2, -1), (8, 9)], lambda p: start_state(cx, st, p))
    for level in (1, 2, 3):
        run([(level - 3, level - 1), (8 - level, 10 - level)], lambda p: advance(cx, st, flux, level, p))
    run([(1, 6)], lambda p: advance(cx, st, flux, 4, p))
    run([(2, 5)], lambda p: advance(cx, st, flux, 5, p))
    run([(3, 4)], lambda p: advance(cx, st, flux, 6, p))
    for n, (level, low_plane, high_plane) in enumerate(EDGES):
        for f in range(10):
            low[n * 10 + f] = st[level * 10 + f, low_plane + 3]
            high[n * 10 + f] = st[level * 10 + f, high_plane + 3]


EDGES = ((3, 0, 6), (3, 1, 7), (4, 1, 5), (4, 2, 6), (5, 2, 5))


def last_kernel(
    flux, weights, got_low, got_high, cx, st_in, hit_row, hit_lane, spot, extra, owner_hit, st, out, packet, final, sems
):
    del st_in
    for n, (level, low_plane, high_plane) in enumerate(EDGES):
        for f in range(10):
            st[level * 10 + f, low_plane + 8 + 3] = got_high[n * 10 + f]
            st[level * 10 + f, high_plane - 8 + 3] = got_low[n * 10 + f]
    run([(-1, 0), (7, 8)], lambda p: advance(cx, st, flux, 4, p))
    run([(-2, 1), (6, 9)], lambda p: advance(cx, st, flux, 5, p))
    run([(-2, 2), (5, 9)], lambda p: advance(cx, st, flux, 6, p))
    run([(-1, 8)], lambda p: advance(cx, st, flux, 7, p))
    run([(0, 7)], lambda p: advance(cx, st, flux, 8, p, out=final))
    copies = [
        pltpu.make_async_copy(final.at[:, :, j, :], out.at[:, :, j * LANES : (j + 1) * LANES], sems.at[0])
        for j in range(8)
    ]
    for copy in copies:
        copy.start()
    press = []
    for r in range(2):
        acc = None
        for j in range(5):
            term = weights[j] * final[r * 5 + j].reshape(64, LANES)
            acc = term if acc is None else acc + term
        press.append(acc)
    rows = hit_row[...]
    lanes = hit_lane[...]
    value = []
    for r in range(2):
        picked = jnp.dot(rows, press[r], precision=HI, preferred_element_type=F32)
        value.append(jnp.sum(picked * lanes, axis=1, keepdims=True))
    column = lax.broadcasted_iota(jnp.int32, spot.shape, 1)
    routed = jnp.where(column < 8, value[0], value[1]) * spot[...] + extra[...]
    packet[...] = jnp.dot(owner_hit[...], routed, precision=HI, preferred_element_type=F32)
    for copy in copies:
        copy.wait()


def as_column(row):
    return jnp.broadcast_to(row.astype(F32), (LANES, row.shape[1])).T.astype(jnp.int32)


def route_kernel(slot_row, cell_row, hit_row, hit_lane, spot, extra, owner_hit):
    rows = slot_row.shape[1]
    owners = owner_hit.shape[0]
    slots = as_column(slot_row[...])
    slot_owner = slots // rows
    owner_col = slot_owner[:, 0:1]
    owner_row = slot_row[...] // rows
    before = lax.broadcasted_iota(jnp.int32, (rows, rows), 1) < lax.broadcasted_iota(jnp.int32, (rows, rows), 0)
    earlier = jnp.where((owner_col == owner_row) & before, 1.0, 0.0)
    position = jnp.sum(earlier, axis=1, keepdims=True).astype(jnp.int32)
    lane = lax.broadcasted_iota(jnp.int32, (rows, LANES), 1)
    here = (lane % 8) == position
    spot[...] = jnp.where(here & (lane < 16), 1.0, 0.0)
    local = (slots - slot_owner * rows).astype(F32)
    extra[...] = jnp.where(here & (lane >= 16) & (lane < 24), local, 0.0)
    owner_hit[...] = jnp.where(lax.broadcasted_iota(jnp.int32, (owners, rows), 0) == owner_row, 1.0, 0.0)
    cells = as_column(cell_row[...])
    hit_row[...] = jnp.where(lane == cells // LANES, 1.0, 0.0)[:, 0:64]
    hit_lane[...] = jnp.where(lane == cells % LANES, 1.0, 0.0)


def force_kernel(arrived, modes_t, shares):
    count = modes_t.shape[1]
    places = lax.broadcasted_iota(jnp.int32, (64, count), 1)
    got = arrived[...]
    re = jnp.zeros((64, count), F32)
    im = jnp.zeros((64, count), F32)
    for i in range(8):
        hit = got[:, 16 + i : 17 + i].astype(jnp.int32) == places
        re = jnp.where(hit, got[:, i : i + 1], re)
        im = jnp.where(hit, got[:, 8 + i : 9 + i], im)
    re = jnp.sum(re, axis=0, keepdims=True)
    im = jnp.sum(im, axis=0, keepdims=True)
    both = jnp.where(lax.broadcasted_iota(jnp.int32, (8, count), 0) < 3, re, im)
    force = lax.dot_general(modes_t[...], both, (((1,), (1,)), ((), ())), precision=HI, preferred_element_type=F32)
    mode = lax.broadcasted_iota(jnp.int32, force.shape, 0)
    column = lax.broadcasted_iota(jnp.int32, force.shape, 1)
    kept = jnp.where((mode % 3 == column % 3) & (column < 6), force, 0.0)
    modes_n = force.shape[0]
    owner = lax.broadcasted_iota(jnp.int32, (64, modes_n), 0)
    mine = jnp.where(lax.broadcasted_iota(jnp.int32, (64, modes_n), 1) // 3 == owner, 1.0, 0.0)
    shares[...] = jnp.zeros(shares.shape, F32)
    shares[:, 0:8] = jnp.dot(mine, kept, precision=HI, preferred_element_type=F32)


def total_kernel(arrived, forces):
    total = jnp.sum(arrived[...], axis=0, keepdims=True)
    forces[0:1, :] = total[:, 0:3]
    forces[1:2, :] = total[:, 3:6]


def call(kernel, outs, ins, scratch=(), aliases=None, cost=None, vmem=24 * MIB):
    return pl.pallas_call(
        kernel,
        out_shape=[jax.ShapeDtypeStruct(shape, F32) for shape, _ in outs],
        in_specs=[pl.BlockSpec(memory_space=space) for _, space in ins],
        out_specs=[pl.BlockSpec(memory_space=space) for _, space in outs],
        scratch_shapes=list(scratch),
        input_output_aliases=aliases or {},
        compiler_params=pltpu.CompilerParams(vmem_limit_bytes=vmem),
        cost_estimate=pl.CostEstimate(flops=cost or 1000000, bytes_accessed=1000, transcendentals=0),
        interpret=INTERPRET,
    )(*[array for array, _ in ins])


V, S, A = pltpu.VMEM, pltpu.SMEM, pl.ANY


def exchange(low, high):
    count = lax.axis_size("space")
    up = [(i, i + 1) for i in range(count - 1)]
    down = [(target, source) for source, target in up]
    return lax.ppermute(high, "space", up), lax.ppermute(low, "space", down)


def local(rhs, inv_diag, face_coef, flux_jac, press_weights, surface_cells, interface_slot, mode_shapes):
    rhs_f = pltpu.with_memory_space_constraint(rhs.reshape(10, 8, 1024), pltpu.HBM)
    inv_f = pltpu.with_memory_space_constraint(inv_diag.reshape(50, 8, 1024), pltpu.HBM)
    face_coef = pltpu.with_memory_space_constraint(face_coef, pltpu.HBM)
    flux = flux_jac
    rows = interface_slot.shape[0]
    dma = pltpu.SemaphoreType.DMA

    low, high = call(
        pack_kernel,
        [((NF + 5, 2, 8, LANES), V)] * 2,
        [(rhs_f, A), (inv_f, A), (face_coef, A)],
        [pltpu.VMEM((60, 2, 8, LANES), F32), dma((2,))],
    )
    got_low, got_high = exchange(low, high)

    hit_row, hit_lane, spot, extra, owner_hit = call(
        route_kernel,
        [((rows, 64), V), ((rows, LANES), V), ((rows, LANES), V), ((rows, LANES), V), ((64, rows), V)],
        [(interface_slot.reshape(1, rows), V), (surface_cells.reshape(1, rows), V)],
    )
    cx, st = call(
        inner_kernel,
        [((NF, 12, 8, LANES), V), ((80, 14, 8, LANES), V)],
        [(flux, S), (rhs_f, A), (inv_f, A), (face_coef, A)],
        [dma((1,))],
    )
    cx, st, low, high = call(
        middle_kernel,
        [((NF, 12, 8, LANES), V), ((80, 14, 8, LANES), V), ((50, 8, LANES), V), ((50, 8, LANES), V)],
        [(flux, S), (got_low, V), (got_high, V), (cx, V), (st, V)],
        aliases={3: 0, 4: 1},
    )
    got_low, got_high = exchange(low, high)
    _, state, packet = call(
        last_kernel,
        [((80, 14, 8, LANES), V), ((10, 8, 1024), A), ((64, LANES), V)],
        [(flux, S), (press_weights, S), (got_low, V), (got_high, V), (cx, V), (st, V), (hit_row, V), (hit_lane, V), (spot, V), (extra, V), (owner_hit, V)],
        [pltpu.VMEM((10, 8, 8, LANES), F32), dma((1,))],
        aliases={5: 0},
    )
    arrived = lax.all_to_all(packet.reshape(64, 1, LANES), "space", 0, 0, tiled=True)
    (shares,) = call(force_kernel, [((64, LANES), V)], [(arrived.reshape(64, LANES), V), (mode_shapes.T, V)])
    arrived = lax.all_to_all(shares.reshape(64, 1, LANES), "space", 0, 0, tiled=True)
    (forces,) = call(total_kernel, [((2, 3), V)], [(arrived.reshape(64, LANES), V)])
    return state.reshape(2, 5, 8, 1024), forces


def solution(mesh):
    in_specs = (
        P(None, None, ("freq", "space"), None),
        P(None, None, None, ("freq", "space"), None),
        P(None, ("freq", "space"), None),
        P(),
        P(),
        P("space"),
        P("space"),
        P("space", None),
    )
    out_specs = (P(None, None, ("freq", "space"), None), P(None, ("freq", "space")))
    return jax.shard_map(local, mesh=mesh, in_specs=in_specs, out_specs=out_specs, check_vma=False)
```

```python
import jax
import jax.numpy as jnp
from jax import lax
from jax.experimental import pallas as pl
from jax.experimental.pallas import tpu as pltpu
from jax.sharding import PartitionSpec as P


INTERPRET = False
HI = lax.Precision.HIGHEST
F32 = jnp.float32
RHS = 50
FAC = 60
NF = 64
LANES = 128
MIB = 1 << 20


def tile_iota(dim):
    return lax.broadcasted_iota(jnp.int32, (8, LANES), dim)


def matvec(blk, vec):
    out = []
    for r in range(2):
        for k in range(5):
            acc = None
            for j in range(5):
                br, bi = blk(k * 5 + j), blk(25 + k * 5 + j)
                if r == 0:
                    term = br * vec[j] - bi * vec[5 + j]
                else:
                    term = br * vec[5 + j] + bi * vec[j]
                acc = term if acc is None else acc + term
            out.append(acc)
    return out


def next_cell(x):
    rolled = pltpu.roll(x, LANES - 1, 1)
    return jnp.where(tile_iota(1) == LANES - 1, pltpu.roll(rolled, 7, 0), rolled)


def prev_cell(x):
    rolled = pltpu.roll(x, 1, 1)
    return jnp.where(tile_iota(1) == 0, pltpu.roll(rolled, 1, 0), rolled)


def start_state(cx, st, planes):
    for plane in planes:
        c, e = plane + 2, plane + 3
        new = matvec(lambda f: cx[f, c], [cx[RHS + f, c] for f in range(10)])
        for f in range(10):
            st[f, e] = new[f]


def advance(cx, st, flux, level, planes, out=None):
    base = (level - 1) * 10
    last = (tile_iota(0) == 7) & (tile_iota(1) == LANES - 1)
    first = (tile_iota(0) == 0) & (tile_iota(1) == 0)
    for plane in planes:
        c, e = plane + 2, plane + 3
        f0, f1, f2, f3 = [cx[FAC + n, c] for n in range(4)]
        f2 = jnp.where(last, 0.0, f2)
        f3 = jnp.where(first, 0.0, f3)
        vec = []
        for r in range(2):
            across, along = [], []
            for j in range(5):
                n = base + r * 5 + j
                here = st[n, e]
                across.append(f0 * st[n, e + 1] + f1 * st[n, e - 1])
                along.append(f2 * next_cell(here) + f3 * prev_cell(here))
            for k in range(5):
                acc = cx[RHS + r * 5 + k, c]
                for j in range(5):
                    acc = acc + flux[0, k, j] * across[j]
                for j in range(5):
                    acc = acc + flux[1, k, j] * along[j]
                vec.append(acc)
        new = matvec(lambda f: cx[f, c], vec)
        for f in range(10):
            if out is None:
                st[level * 10 + f, e] = new[f]
            else:
                out[f, plane] = new[f]


def run(low, high, body):
    if low == high:
        body((low, 7 - low))
    else:

        @pl.loop(low, high + 1)
        def _(plane):
            body((plane, 7 - plane))


def plane_copies(source, target, sems, first, count, offset, at):
    copies = []
    for j in range(8):
        copies.append(
            pltpu.make_async_copy(
                source.at[:, first : first + count, j * LANES : (j + 1) * LANES],
                target.at[offset : offset + source.shape[0], at : at + count, j, :],
                sems,
            )
        )
    return copies


def pack_kernel(rhs, inv, face, low, high, edge, sems):
    copies = []
    for side, (target, first, inner) in enumerate(((low, 0, 2), (high, 6, 5))):
        copies += plane_copies(inv, target, sems.at[side], first, 2, 0, 0)
        copies += plane_copies(rhs, target, sems.at[side], first, 2, RHS, 0)
        copies += plane_copies(face, target, sems.at[side], first, 2, FAC, 0)
        copies += plane_copies(inv, edge, sems.at[side], inner, 1, 0, side)
        copies += plane_copies(rhs, edge, sems.at[side], inner, 1, RHS, side)
    for copy in copies:
        copy.start()
    for copy in copies:
        copy.wait()
    for side, target in enumerate((low, high)):
        new = matvec(lambda f: edge[f, side], [edge[RHS + f, side] for f in range(10)])
        for f in range(10):
            target[NF + f // 2, f % 2] = new[f]


def inner_kernel(flux, rhs, inv, face, cx, st, sems):
    copies = (
        plane_copies(inv, cx, sems.at[0], 0, 8, 0, 2)
        + plane_copies(rhs, cx, sems.at[0], 0, 8, RHS, 2)
        + plane_copies(face, cx, sems.at[0], 0, 8, FAC, 2)
    )
    for copy in copies:
        copy.start()
    for copy in copies:
        copy.wait()
    run(0, 3, lambda p: start_state(cx, st, p))
    for level in (1, 2, 3):
        run(level, 3, lambda p: advance(cx, st, flux, level, p))


def middle_kernel(flux, got_low, got_high, cx_in, st_in, cx, st, low, high, mid):
    del cx_in, st_in
    @pl.loop(0, NF)
    def _(f):
        for p in range(2):
            cx[f, p] = got_low[f, p]
            cx[f, 10 + p] = got_high[f, p]

    for f in range(10):
        st[f, 0] = got_low[NF + f // 2, f % 2]
        st[f, 13] = got_high[NF + f // 2, f % 2]
    run(-2, -1, lambda p: start_state(cx, st, p))
    for level in (1, 2, 3):
        run(level - 3, level - 1, lambda p: advance(cx, st, flux, level, p))
    run(1, 3, lambda p: advance(cx, st, flux, 4, p))
    run(2, 3, lambda p: advance(cx, st, flux, 5, p))
    run(3, 3, lambda p: advance(cx, st, flux, 6, p))
    for n, (level, low_plane, high_plane) in enumerate(EDGES):
        for f in range(10):
            low[n * 10 + f] = st[level * 10 + f, low_plane + 3]
            high[n * 10 + f] = st[level * 10 + f, high_plane + 3]
    for n, (level, plane) in enumerate(MIDDLE):
        for f in range(10):
            mid[n * 10 + f] = st[level * 10 + f, plane + 3]


EDGES = ((3, 0, 6), (3, 1, 7), (4, 1, 5), (4, 2, 6), (5, 2, 5))
MIDDLE = ((5, 3), (5, 4), (6, 3), (6, 4))


def last_kernel(
    flux, weights, got_low, got_high, low, high, mid, cx, ordered, out, value, st, final, sems
):
    for n, (level, low_plane, high_plane) in enumerate(EDGES):
        for f in range(10):
            at = (level - 3) * 10 + f
            st[at, low_plane + 8 + 3] = got_high[n * 10 + f]
            st[at, high_plane - 8 + 3] = got_low[n * 10 + f]
            st[at, low_plane + 3] = low[n * 10 + f]
            st[at, high_plane + 3] = high[n * 10 + f]
    for n, (level, plane) in enumerate(MIDDLE):
        for f in range(10):
            st[(level - 3) * 10 + f, plane + 3] = mid[n * 10 + f]
    run(-1, 0, lambda p: advance(cx, st, flux, 1, p))
    run(-2, 1, lambda p: advance(cx, st, flux, 2, p))
    run(-2, 2, lambda p: advance(cx, st, flux, 3, p))
    run(-1, 3, lambda p: advance(cx, st, flux, 4, p))
    run(0, 3, lambda p: advance(cx, st, flux, 5, p, out=final))
    copies = [
        pltpu.make_async_copy(final.at[:, :, j, :], out.at[:, :, j * LANES : (j + 1) * LANES], sems.at[0])
        for j in range(8)
    ]
    for copy in copies:
        copy.start()
    press = []
    for r in range(2):
        acc = None
        for j in range(5):
            term = weights[j] * final[r * 5 + j].reshape(64, LANES)
            acc = term if acc is None else acc + term
        press.append(acc)
    cells = as_column(ordered[0:1, :])
    lane = lax.broadcasted_iota(jnp.int32, cells.shape, 1)
    rows = jnp.where(lane == cells // LANES, 1.0, 0.0)[:, 0:64]
    column = []
    for r in range(2):
        picked = jnp.dot(rows, press[r], precision=HI, preferred_element_type=F32)
        column.append(jnp.sum(jnp.where(lane == cells % LANES, picked, 0.0), axis=1, keepdims=True))
    value[...] = jnp.where(lane == 0, column[0], column[1]).T[0:8, :]
    for copy in copies:
        copy.wait()


def as_column(row):
    return jnp.broadcast_to(row.astype(F32), (LANES, row.shape[1])).T.astype(jnp.int32)


def route_kernel(slot_row, cell_row, ordered, wanted):
    slots, cells = slot_row[...], cell_row[...]
    rows = slots.shape[1]
    owners = wanted.shape[0]
    share = rows // owners
    owner = slots // rows
    local = (slots - owner * rows).astype(F32)
    below = lax.broadcasted_iota(jnp.int32, (rows, rows), 0)
    across = lax.broadcasted_iota(jnp.int32, (rows, rows), 1)
    earlier = jnp.where((as_column(owner)[:, 0:1] == owner) & (below < across), 1.0, 0.0)
    place = jnp.sum(earlier, axis=0, keepdims=True).astype(jnp.int32)
    move = jnp.where(owner * share + place == below, cells.astype(F32), 0.0)
    move = jnp.sum(move, axis=1, keepdims=True)
    ordered[...] = jnp.broadcast_to(move, (rows, LANES)).T[0:8, :]
    by_owner = jnp.where(lax.broadcasted_iota(jnp.int32, (owners, rows), 0) == owner, 1.0, 0.0)
    by_place = jnp.where(lax.broadcasted_iota(jnp.int32, (8, rows), 0) == place, local, 0.0)
    wanted[...] = jnp.zeros(wanted.shape, F32)
    wanted[:, 0:8] = lax.dot_general(
        by_owner, by_place, (((1,), (1,)), ((), ())), precision=HI, preferred_element_type=F32
    )


def gather_kernel(asked, modes_t, rows_out):
    count = modes_t.shape[1]
    modes_n = modes_t.shape[0]
    places = lax.broadcasted_iota(jnp.int32, (64, count), 1)
    got = asked[...]
    rows_out[...] = jnp.zeros(rows_out.shape, F32)
    for i in range(8):
        hit = jnp.where(got[:, i : i + 1].astype(jnp.int32) == places, 1.0, 0.0)
        rows_out[:, i, 0:modes_n] = lax.dot_general(
            hit, modes_t[...], (((1,), (1,)), ((), ())), precision=HI, preferred_element_type=F32
        )


def force_kernel(value, rows_in, shares):
    rows = rows_in[...].reshape(512, 256)
    total = []
    column = value[...].T
    for r in range(2):
        total.append(jnp.sum(rows * column[:, r : r + 1], axis=0, keepdims=True))
    line = lax.broadcasted_iota(jnp.int32, (8, 256), 0)
    mode = lax.broadcasted_iota(jnp.int32, (8, 256), 1)
    kept = jnp.where((mode % 3 == line % 3) & (line < 6), jnp.where(line < 3, total[0], total[1]), 0.0)
    mine = lax.broadcasted_iota(jnp.int32, (64, 256), 1) // 3 == lax.broadcasted_iota(jnp.int32, (64, 256), 0)
    shares[...] = jnp.zeros(shares.shape, F32)
    shares[:, 0:8] = lax.dot_general(
        jnp.where(mine, 1.0, 0.0), kept, (((1,), (1,)), ((), ())), precision=HI, preferred_element_type=F32
    )


def total_kernel(arrived, forces):
    total = jnp.sum(arrived[...], axis=0, keepdims=True)
    forces[0:1, :] = total[:, 0:3]
    forces[1:2, :] = total[:, 3:6]


def call(kernel, outs, ins, scratch=(), aliases=None, cost=None, vmem=24 * MIB):
    return pl.pallas_call(
        kernel,
        out_shape=[jax.ShapeDtypeStruct(shape, F32) for shape, _ in outs],
        in_specs=[pl.BlockSpec(memory_space=space) for _, space in ins],
        out_specs=[pl.BlockSpec(memory_space=space) for _, space in outs],
        scratch_shapes=list(scratch),
        input_output_aliases=aliases or {},
        compiler_params=pltpu.CompilerParams(vmem_limit_bytes=vmem),
        cost_estimate=pl.CostEstimate(flops=cost or 1000000, bytes_accessed=1000, transcendentals=0),
        interpret=INTERPRET,
    )(*[array for array, _ in ins])


V, S, A = pltpu.VMEM, pltpu.SMEM, pl.ANY


def exchange(low, high):
    count = lax.axis_size("space")
    up = [(i, i + 1) for i in range(count - 1)]
    down = [(target, source) for source, target in up]
    return lax.ppermute(high, "space", up), lax.ppermute(low, "space", down)


def trade(parts):
    return lax.all_to_all(parts, "space", 0, 0, tiled=True)


def program(rhs, inv_diag, face_coef, flux_jac, press_weights, surface_cells, interface_slot, mode_shapes):
    rhs_f = pltpu.with_memory_space_constraint(rhs.reshape(10, 8, 1024), pltpu.HBM)
    inv_f = pltpu.with_memory_space_constraint(inv_diag.reshape(50, 8, 1024), pltpu.HBM)
    face_coef = pltpu.with_memory_space_constraint(face_coef, pltpu.HBM)
    flux = flux_jac
    rows = interface_slot.shape[0]
    dma = pltpu.SemaphoreType.DMA

    low, high = call(
        pack_kernel,
        [((NF + 5, 2, 8, LANES), V)] * 2,
        [(rhs_f, A), (inv_f, A), (face_coef, A)],
        [pltpu.VMEM((60, 2, 8, LANES), F32), dma((2,))],
    )
    got_low, got_high = exchange(low, high)

    ordered, wanted = call(
        route_kernel,
        [((8, rows), V), ((64, LANES), V)],
        [(interface_slot.reshape(1, rows), V), (surface_cells.reshape(1, rows), V)],
    )
    asked = trade(wanted.reshape(64, 1, LANES)).reshape(64, LANES)
    cx, st = call(
        inner_kernel,
        [((NF, 12, 8, LANES), V), ((70, 14, 8, LANES), V)],
        [(flux, S), (rhs_f, A), (inv_f, A), (face_coef, A)],
        [dma((1,))],
    )
    cx, st, low, high, mid = call(
        middle_kernel,
        [((NF, 12, 8, LANES), V), ((70, 14, 8, LANES), V), ((50, 8, LANES), V), ((50, 8, LANES), V), ((40, 8, LANES), V)],
        [(flux, S), (got_low, V), (got_high, V), (cx, V), (st, V)],
        aliases={3: 0, 4: 1},
    )
    got_low, got_high = exchange(low, high)
    (mode_rows,) = call(gather_kernel, [((64, 8, 256), V)], [(asked, V), (mode_shapes.T, V)])
    mode_rows = trade(mode_rows)
    state, value = call(
        last_kernel,
        [((10, 8, 1024), A), ((8, rows), V)],
        [(flux, S), (press_weights, S), (got_low, V), (got_high, V), (low, V), (high, V), (mid, V), (cx, V), (ordered, V)],
        [pltpu.VMEM((50, 14, 8, LANES), F32), pltpu.VMEM((10, 8, 8, LANES), F32), dma((1,))],
    )
    (shares,) = call(force_kernel, [((64, LANES), V)], [(value, V), (mode_rows, V)])
    arrived = trade(shares.reshape(64, 1, LANES))
    (forces,) = call(total_kernel, [((2, 3), V)], [(arrived.reshape(64, LANES), V)])
    return state.reshape(2, 5, 8, 1024), forces


def solution(mesh):
    in_specs = (
        P(None, None, ("freq", "space"), None),
        P(None, None, None, ("freq", "space"), None),
        P(None, ("freq", "space"), None),
        P(),
        P(),
        P("space"),
        P("space"),
        P("space", None),
    )
    out_specs = (P(None, None, ("freq", "space"), None), P(None, ("freq", "space")))
    return jax.shard_map(program, mesh=mesh, in_specs=in_specs, out_specs=out_specs, check_vma=False)
```
